32 devices in a mesh: groups: 2 (over y), ctx: 4 (over z), tp: 4 (over x, core).
Axes of the slice: x: 2, y: 2, z: 4, core: 2. Of those that a mesh axis runs over, the one named last changes fastest.
Arguments:
- queries: bfloat16 [2048, 5120], P(('groups', 'ctx'), 'tp'), parts along dimension 0, may hold values from -16 to 16
- keys: bfloat16 [2048, 1024], P(('groups', 'ctx'), 'tp'), parts along dimension 0, may hold values from -16 to 16
- values: bfloat16 [2048, 1024], P(('groups', 'ctx'), 'tp'), parts along dimension 0, may hold values from -6 to 6
- positions: int32 [2048], P('groups'), parts along dimension 0, may hold values from 0 to 1023, as said below
- out_weight: bfloat16 [5120, 5120], P('tp', 'ctx'), may hold values from -0.59765625 to 0.59765625
Outputs:
- mixed: bfloat16 [2048, 5120], P(('groups', 'ctx'), 'tp'), parts along dimension 0
The draws below stay inside these ranges and needn't reach their ends.
There are 2 independent parts, one for each index of `groups`. The reference program is written for one: setup_inputs(seed, part) draws one part's arguments, and reference() takes and returns one part's arrays. A program takes and returns all parts, laid end to end along the dimension named above; an argument that names none is the same for every part. Nothing has to cross between parts.
Inputs may be any that keep to these rules, and one draw needn't show every extreme that they name: positions is a permutation of all positions made of 8 aligned runs of 128 consecutive positions, each run increasing.
All inputs are finite; a program needn't handle non-finite values.
Results may differ from the reference program's by a relative error of at most 0.0095.
Values may be sent and summed in bfloat16 or wider, within the bound.
No kernel may reach another device: no remote copies, remote signals or barrier semaphores. Data moves between devices by JAX's collectives and lax.ppermute only.
A program may use at most 64 MiB of HBM per device.

```python
import jax
import jax.numpy as jnp
from jax import lax

D = 5120
QUERY_HEADS = 40
KEY_VALUE_HEADS = 8
HEAD_SIZE = 128
TOK_DEV = 256
SEQUENCE_TOKENS = 1024
BLOCK = 128
NBLK = 8
N_TP = 4


def block_order(key):
    return jax.random.permutation(jax.random.fold_in(key, 101), NBLK).astype(jnp.int32)


def position_table(key):
    order = block_order(key)
    within = jnp.arange(BLOCK, dtype=jnp.int32)
    return (order[:, None] * BLOCK + within[None, :]).reshape(SEQUENCE_TOKENS).astype(jnp.int32)


def draw_positions(key, part):
    return position_table(key)


def starting_values(key, rows, cols, salt):
    inner = jax.random.fold_in(key, salt)
    return jnp.clip(jax.random.normal(inner, (rows, cols), jnp.float32), -6.0, 6.0)


def draw_queries(key, part):
    final_output = starting_values(key, SEQUENCE_TOKENS, QUERY_HEADS * HEAD_SIZE, 303)
    return jnp.clip(final_output, -16.0, 16.0).astype(jnp.bfloat16)


def draw_keys(key, part):
    final_output = starting_values(key, SEQUENCE_TOKENS, KEY_VALUE_HEADS * HEAD_SIZE, 404)
    return jnp.clip(final_output, -16.0, 16.0).astype(jnp.bfloat16)


def level_of(own_key, dims, shards, low, top_value):
    def one(axis_at, blocks):
        heights = jax.random.uniform(jax.random.fold_in(jax.random.fold_in(own_key, 6), axis_at), (blocks,), jnp.float32, low / len(shards), top_value / len(shards))
        return jnp.repeat(jnp.exp(heights), dims[axis_at] // blocks).reshape((-1,) + (1,) * (len(dims) - axis_at - 1))

    level = one(*shards[0])
    for cut in shards[1:]:
        level = level * one(*cut)
    return level


def normal_values(stream_key, dims, scale, bound, split=(), kind=jnp.bfloat16):
    values = scale * jax.random.normal(stream_key, dims, jnp.float32)
    if split:
        values = values * level_of(stream_key, dims, split, -0.22, 0.18)
    return jnp.clip(values, -bound, bound).astype(kind)


def setup_inputs(seed: int = 0, part: int = 0) -> dict:
    streams_of = jax.random.split(jax.random.key(seed), 6)
    own_keys = jax.random.split(jax.random.fold_in(streams_of[5], part), 6)
    return {
        "queries": draw_queries(jax.random.fold_in(jax.random.fold_in(streams_of[5], part), 71), part),
        "keys": draw_keys(jax.random.fold_in(jax.random.fold_in(streams_of[5], part), 71), part),
        "values": normal_values(own_keys[2], (SEQUENCE_TOKENS, KEY_VALUE_HEADS * HEAD_SIZE), 1.0, 6.0, ((0, 4), (1, 4))),
        "positions": draw_positions(jax.random.fold_in(jax.random.fold_in(streams_of[5], part), 71), part),
        "out_weight": normal_values(streams_of[4], (QUERY_HEADS * HEAD_SIZE, D), 0.1, 0.59765625, ((0, 4), (1, 4))),
    }


def reference(queries, keys, values, positions, out_weight):
    query_group = QUERY_HEADS // KEY_VALUE_HEADS
    scale = HEAD_SIZE ** -0.5
    query_heads = queries.reshape(SEQUENCE_TOKENS, QUERY_HEADS, HEAD_SIZE).transpose(1, 0, 2)
    key_head_rows = jnp.repeat(keys.reshape(SEQUENCE_TOKENS, KEY_VALUE_HEADS, HEAD_SIZE).transpose(1, 0, 2), query_group, axis=0)
    value_head_rows = jnp.repeat(values.reshape(SEQUENCE_TOKENS, KEY_VALUE_HEADS, HEAD_SIZE).transpose(1, 0, 2), query_group, axis=0)
    row_count = SEQUENCE_TOKENS // TOK_DEV
    query_pos = positions.reshape(row_count, TOK_DEV)

    def head_fn(items):
        q_all, k_all, v_all = items
        q_rows = q_all.reshape(row_count, TOK_DEV, HEAD_SIZE)

        def row_fn(pair):
            q_block, pos_block = pair
            scores = jnp.dot(q_block, k_all.T, preferred_element_type=jnp.float32) * scale
            keep = positions[None, :] <= pos_block[:, None]
            scores = jnp.where(keep, scores, -jnp.inf)
            top = jnp.max(scores, axis=1, keepdims=True)
            expo = jnp.where(keep, jnp.exp(scores - top), 0.0)
            total = jnp.sum(expo, axis=1, keepdims=True)
            weights = expo.astype(jnp.bfloat16)
            final_output = jnp.dot(weights, v_all, preferred_element_type=jnp.float32) / total
            return final_output.astype(jnp.bfloat16)

        return lax.map(row_fn, (q_rows, query_pos)).reshape(SEQUENCE_TOKENS, HEAD_SIZE)

    attended = lax.map(head_fn, (query_heads, key_head_rows, value_head_rows))
    attended = attended.transpose(1, 0, 2).reshape(SEQUENCE_TOKENS, QUERY_HEADS * HEAD_SIZE)
    width = QUERY_HEADS * HEAD_SIZE // N_TP
    summed = jnp.zeros((SEQUENCE_TOKENS, D), jnp.float32)
    for index in range(N_TP):
        cols = attended[:, index * width:(index + 1) * width]
        rows = out_weight[index * width:(index + 1) * width, :]
        partial_value = jnp.dot(cols, rows, preferred_element_type=jnp.float32).astype(jnp.bfloat16)
        partial_value = lax.optimization_barrier(partial_value)
        summed = summed + partial_value.astype(jnp.float32)
    return summed.astype(jnp.bfloat16)
```

```python
import functools
import math

import jax
import jax.numpy as jnp
from jax import lax
from jax.experimental import pallas as pl
from jax.experimental.pallas import tpu as pltpu
from jax.sharding import PartitionSpec as P

QUERY_HEADS = 40
KEY_VALUE_HEADS = 8
HEAD_SIZE = 128


def attend_kernel(qpos_ref, kpos_ref, q_ref, *refs, group, slots):
    k_refs, v_refs, o_ref = refs[:slots], refs[slots : 2 * slots], refs[2 * slots]
    rows = q_ref.shape[0]
    heads = [q_ref[:, h * HEAD_SIZE : (h + 1) * HEAD_SIZE] for h in range(group)]
    query = jnp.concatenate(heads, axis=0)
    scale = HEAD_SIZE ** (-0.5)
    query_pos = qpos_ref[...]
    scores = []
    for i in range(slots):
        part = lax.dot_general(
            query, k_refs[i][...], (((1,), (1,)), ((), ())), preferred_element_type=jnp.float32
        )
        count = part.shape[1]
        keep = kpos_ref[:, i * count : (i + 1) * count] <= query_pos
        part = part.reshape(group, rows, count) * scale
        scores.append(jnp.where(keep[None], part, -1e30))
    top = functools.reduce(jnp.maximum, [jnp.max(s, axis=-1, keepdims=True) for s in scores])
    total = 0.0
    accum = 0.0
    for i in range(slots):
        expo = jnp.exp(scores[i] - top)
        total = total + jnp.sum(expo, axis=-1, keepdims=True)
        weights = expo.astype(jnp.bfloat16).reshape(group * rows, -1)
        accum = accum + jnp.dot(weights, v_refs[i][...], preferred_element_type=jnp.float32)
    result = (accum.reshape(group, rows, HEAD_SIZE) / total).astype(jnp.bfloat16)
    for h in range(group):
        o_ref[:, h * HEAD_SIZE : (h + 1) * HEAD_SIZE] = result[h]


def attend(queries, kv_slots, query_pos, key_pos):
    tok, width = queries.shape
    count = kv_slots[0].shape[0]
    kv_heads = kv_slots[0].shape[1] // (2 * HEAD_SIZE)
    group = width // (kv_heads * HEAD_SIZE)
    slots = len(kv_slots)
    k_spec = pl.BlockSpec((count, HEAD_SIZE), lambda g: (0, g))
    v_spec = pl.BlockSpec((count, HEAD_SIZE), lambda g: (0, kv_heads + g))
    q_spec = pl.BlockSpec((tok, group * HEAD_SIZE), lambda g: (0, g))
    pairs = tok * count * slots * kv_heads * group
    return pl.pallas_call(
        functools.partial(attend_kernel, group=group, slots=slots),
        out_shape=jax.ShapeDtypeStruct((tok, width), jnp.bfloat16),
        grid=(kv_heads,),
        in_specs=[
            pl.BlockSpec((tok, 1), lambda g: (0, 0)),
            pl.BlockSpec((1, slots * count), lambda g: (0, 0)),
            q_spec,
        ]
        + [k_spec] * slots
        + [v_spec] * slots,
        out_specs=q_spec,
        cost_estimate=pl.CostEstimate(
            flops=4 * pairs * HEAD_SIZE, bytes_accessed=4 * tok * width, transcendentals=pairs
        ),
        name="attend",
    )(query_pos.reshape(tok, 1), key_pos.reshape(1, -1), queries, *kv_slots, *kv_slots)


def project_kernel(a_ref, b_ref, wa_ref, wb_ref, o_ref):
    accum = jnp.dot(a_ref[...], wa_ref[...], preferred_element_type=jnp.float32)
    accum = accum + jnp.dot(b_ref[...], wb_ref[...], preferred_element_type=jnp.float32)
    o_ref[...] = accum.astype(jnp.bfloat16)


def project(a, b, wa, wb, tile=256):
    rows, depth = a.shape
    cols = wa.shape[1]
    a_spec = pl.BlockSpec((rows, depth), lambda n: (0, 0))
    w_spec = pl.BlockSpec((depth, tile), lambda n: (0, n))
    return pl.pallas_call(
        project_kernel,
        out_shape=jax.ShapeDtypeStruct((rows, cols), jnp.bfloat16),
        grid=(cols // tile,),
        in_specs=[a_spec, a_spec, w_spec, w_spec],
        out_specs=pl.BlockSpec((rows, tile), lambda n: (0, n)),
        cost_estimate=pl.CostEstimate(
            flops=4 * rows * depth * cols, bytes_accessed=4 * depth * cols, transcendentals=0
        ),
        name="project",
    )(a, b, wa, wb)


FIRST = [(0, 1), (1, 0), (2, 3), (3, 2)]
MIDDLE = [(1, 2), (2, 1)]
OUTWARD = [(1, 0), (2, 3)]


def xor(step):
    return [(i, i ^ step) for i in range(4)]


def line_gather(block, middle):
    near = lax.ppermute(block, "ctx", FIRST)
    across = lax.ppermute(block, "ctx", MIDDLE)
    far = lax.ppermute(near, "ctx", MIDDLE)
    out_near = lax.ppermute(across, "ctx", OUTWARD)
    out_far = lax.ppermute(far, "ctx", OUTWARD)
    third = jnp.where(middle, across, out_near)
    fourth = jnp.where(middle, far, out_far)
    return near, third, fourth


def four_planes(queries, keys, values, positions, out_weight):
    tok = queries.shape[0]
    half = tok // 2
    c = lax.axis_index("ctx")
    t = lax.axis_index("tp")
    core = t % 2
    middle = (c == 1) | (c == 2)
    other = jnp.where(c < 2, 2, 1)
    order = [c, c ^ 1, other, other ^ 1]

    kv = jnp.concatenate([keys, values], axis=1)
    kv_slots = (kv,) + line_gather(kv, middle)
    pos_of = [lax.dynamic_slice_in_dim(positions, i * tok, tok) for i in order]
    attended = attend(queries, kv_slots, pos_of[0], jnp.concatenate(pos_of))

    weight_pair = lax.ppermute(out_weight, "tp", xor(1))
    mine = lax.dynamic_slice_in_dim(attended, core * half, half)
    theirs = lax.dynamic_slice_in_dim(attended, (1 - core) * half, half)
    given = lax.ppermute(theirs, "tp", xor(1))
    block = jnp.concatenate([mine, given], axis=0)

    near, third, fourth = line_gather(block, middle)

    def projected(parts):
        a = jnp.concatenate([p[:half] for p in parts], axis=0)
        b = jnp.concatenate([p[half:] for p in parts], axis=0)
        return project(a, b, out_weight, weight_pair)

    early = projected([block, near])
    late = projected([third, fourth])
    own, to_near = early[:half], early[half:]
    to_third, to_fourth = late[:half], late[half:]
    two = jnp.where(middle, to_fourth, to_third)
    three = jnp.where(middle, to_third, to_fourth)
    from_one = lax.ppermute(to_near, "ctx", xor(1))
    from_two = lax.ppermute(two, "ctx", xor(2))
    from_three = lax.ppermute(three, "ctx", xor(3))
    by_step = [own, from_one, from_two, from_three]

    def columns(p):
        step = p ^ c
        return jnp.where(
            step < 2,
            jnp.where(step == 0, by_step[0], by_step[1]),
            jnp.where(step == 2, by_step[2], by_step[3]),
        )

    got = [columns(t)] + [lax.ppermute(columns(t ^ j), "tp", xor(j)) for j in (1, 2, 3)]
    f32 = jnp.float32
    same = (got[0].astype(f32) + got[2].astype(f32)).astype(jnp.bfloat16)
    swap = (got[1].astype(f32) + got[3].astype(f32)).astype(jnp.bfloat16)
    top = jnp.where(core == 0, same, swap)
    low = jnp.where(core == 0, swap, same)
    return jnp.concatenate([top, low], axis=0)


def any_mesh(queries, keys, values, positions, out_weight):
    tok = queries.shape[0]
    kv_heads = keys.shape[1] // HEAD_SIZE
    query_group = QUERY_HEADS // KEY_VALUE_HEADS
    scale = HEAD_SIZE ** (-0.5)
    ctx_index = lax.axis_index("ctx")
    query_pos = lax.dynamic_slice_in_dim(positions, ctx_index * tok, tok)
    query_four = queries.reshape(tok, kv_heads, query_group, HEAD_SIZE)

    def attend_block(carry, key_block, value_block, key_pos):
        top, total, accum = carry
        count = key_block.shape[0]
        key_three = key_block.reshape(count, kv_heads, HEAD_SIZE)
        value_three = value_block.reshape(count, kv_heads, HEAD_SIZE)
        scores = (
            jnp.einsum("tgjd,kgd->gjtk", query_four, key_three, preferred_element_type=jnp.float32)
            * scale
        )
        keep = key_pos[None, :] <= query_pos[:, None]
        scores = jnp.where(keep, scores, -1e30)
        new_top = jnp.maximum(top, jnp.max(scores, axis=-1))
        factor = jnp.exp(top - new_top)
        expo = jnp.where(keep, jnp.exp(scores - new_top[..., None]), 0.0)
        total = total * factor + jnp.sum(expo, axis=-1)
        weights = expo.astype(jnp.bfloat16)
        accum = accum * factor[..., None] + jnp.einsum(
            "gjtk,kgd->gjtd", weights, value_three, preferred_element_type=jnp.float32
        )
        return (new_top, total, accum)

    start_top = jnp.full((kv_heads, query_group, tok), -1e30, jnp.float32)
    start_total = jnp.zeros((kv_heads, query_group, tok), jnp.float32)
    start_accum = jnp.zeros((kv_heads, query_group, tok, HEAD_SIZE), jnp.float32)
    key_piece = lax.all_gather(keys, "ctx", axis=0, tiled=True)
    value_piece = lax.all_gather(values, "ctx", axis=0, tiled=True)
    rows = key_piece.shape[0]
    width = math.gcd(rows, 512)

    def step(index, state):
        offset = index * width
        key_block = lax.dynamic_slice_in_dim(key_piece, offset, width, 0)
        value_block = lax.dynamic_slice_in_dim(value_piece, offset, width, 0)
        key_pos = lax.dynamic_slice_in_dim(positions, offset, width, 0)
        return attend_block(state, key_block, value_block, key_pos)

    top, total, accum = lax.fori_loop(0, rows // width, step, (start_top, start_total, start_accum))
    attended = (
        (accum / total[..., None])
        .transpose(2, 0, 1, 3)
        .reshape(tok, kv_heads * query_group * HEAD_SIZE)
        .astype(jnp.bfloat16)
    )
    partial_value = jnp.dot(
        attended,
        lax.all_gather(out_weight, "ctx", axis=1, tiled=True),
        preferred_element_type=jnp.float32,
    )
    return lax.psum_scatter(
        partial_value.astype(jnp.bfloat16), "tp", scatter_dimension=1, tiled=True
    )


def solution(mesh):
    square = mesh.shape["ctx"] == 4 and mesh.shape["tp"] == 4
    return jax.shard_map(
        four_planes if square else any_mesh,
        mesh=mesh,
        in_specs=(
            P(("groups", "ctx"), "tp"),
            P(("groups", "ctx"), "tp"),
            P(("groups", "ctx"), "tp"),
            P("groups"),
            P("tp", "ctx"),
        ),
        out_specs=P(("groups", "ctx"), "tp"),
        check_vma=False,
    )
```

```python
import functools
import math

import jax
import jax.numpy as jnp
from jax import lax
from jax.experimental import pallas as pl
from jax.experimental.pallas import tpu as pltpu
from jax.sharding import PartitionSpec as P


QUERY_HEADS = 40
KEY_VALUE_HEADS = 8
HEAD_SIZE = 128
ATTEND_VMEM = 28 * 2**20


def attend_kernel(order_ref, qpos_ref, kpos_ref, q_ref, *refs, group, slots, pieces):
    k_refs, v_refs = refs[:slots], refs[slots : 2 * slots]
    o_refs, scratch = refs[2 * slots : 2 * slots + pieces], refs[2 * slots + pieces]
    rows = q_ref.shape[0]
    heads = [q_ref[:, h * HEAD_SIZE : (h + 1) * HEAD_SIZE] for h in range(group)]
    query = jnp.concatenate(heads, axis=0)
    scale = HEAD_SIZE ** (-0.5)
    query_pos = qpos_ref[...]
    scores = []
    for i in range(slots):
        part = lax.dot_general(
            query, k_refs[i][...], (((1,), (1,)), ((), ())), preferred_element_type=jnp.float32
        )
        count = part.shape[1]
        keep = kpos_ref[:, i * count : (i + 1) * count] <= query_pos
        part = part.reshape(group, rows, count) * scale
        scores.append(jnp.where(keep[None], part, -1e30))
    top = functools.reduce(jnp.maximum, [jnp.max(s, axis=-1, keepdims=True) for s in scores])
    total = 0.0
    accum = 0.0
    for i in range(slots):
        expo = jnp.exp(scores[i] - top)
        total = total + jnp.sum(expo, axis=-1, keepdims=True)
        weights = expo.astype(jnp.bfloat16).reshape(group * rows, -1)
        accum = accum + jnp.dot(weights, v_refs[i][...], preferred_element_type=jnp.float32)
    result = (accum.reshape(group, rows, HEAD_SIZE) / total).astype(jnp.bfloat16)
    for h in range(group):
        scratch[:, h * HEAD_SIZE : (h + 1) * HEAD_SIZE] = result[h]
    part_rows = rows // pieces
    for i in range(pieces):
        start = pl.multiple_of(order_ref[i] * part_rows, part_rows)
        o_refs[i][...] = scratch[pl.ds(start, part_rows), :]


def attend(queries, kv_slots, query_pos, key_pos, order):
    tok, width = queries.shape
    count = kv_slots[0].shape[0]
    kv_heads = kv_slots[0].shape[1] // (2 * HEAD_SIZE)
    group = width // (kv_heads * HEAD_SIZE)
    slots, pieces = len(kv_slots), order.shape[0]
    k_spec = pl.BlockSpec((count, HEAD_SIZE), lambda g, *_: (0, g))
    v_spec = pl.BlockSpec((count, HEAD_SIZE), lambda g, *_: (0, kv_heads + g))
    q_spec = pl.BlockSpec((tok, group * HEAD_SIZE), lambda g, *_: (0, g))
    o_spec = pl.BlockSpec((tok // pieces, group * HEAD_SIZE), lambda g, *_: (0, g))
    pairs = tok * count * slots * kv_heads * group
    return pl.pallas_call(
        functools.partial(attend_kernel, group=group, slots=slots, pieces=pieces),
        out_shape=[jax.ShapeDtypeStruct((tok // pieces, width), jnp.bfloat16)] * pieces,
        grid_spec=pltpu.PrefetchScalarGridSpec(
            num_scalar_prefetch=1,
            grid=(kv_heads,),
            in_specs=[
                pl.BlockSpec((tok, 1), lambda g, *_: (0, 0)),
                pl.BlockSpec((1, slots * count), lambda g, *_: (0, 0)),
                q_spec,
            ]
            + [k_spec] * slots
            + [v_spec] * slots,
            out_specs=[o_spec] * pieces,
            scratch_shapes=[pltpu.VMEM((tok, group * HEAD_SIZE), jnp.bfloat16)],
        ),
        cost_estimate=pl.CostEstimate(
            flops=4 * pairs * HEAD_SIZE, bytes_accessed=4 * tok * width, transcendentals=pairs
        ),
        compiler_params=pltpu.CompilerParams(vmem_limit_bytes=ATTEND_VMEM),
        name="attend",
    )(order, query_pos.reshape(tok, 1), key_pos.reshape(1, -1), queries, *kv_slots, *kv_slots)


def project_kernel(order_ref, *refs, slots, chunks, base):
    refs, pieces = list(refs), len(chunks)
    sources = [[[refs.pop(0) for _ in range(pieces)] for _ in range(n)] for n in slots]
    w_refs = [[refs.pop(0) for _ in range(n)] for n in chunks]
    accum = refs.pop(0)[...] if base else 0.0
    rest = refs
    rows = sources[0][0][0].shape[0]
    for j in range(pieces):
        part = [functools.reduce(jnp.add, [block[j][...] for block in slot]) for slot in sources]
        part = jnp.concatenate(part, axis=0)
        start = 0
        for w_ref in w_refs[j]:
            stop = start + w_ref.shape[0]
            accum = accum + jnp.dot(
                part[:, start:stop], w_ref[...], preferred_element_type=jnp.float32
            )
            start = stop
    if not base:
        rest[0][...] = accum
        return
    count = len(slots)
    o_refs, scratch = rest[:count], rest[count]
    scratch[...] = accum
    for i in range(count):
        start = pl.multiple_of(order_ref[i] * rows, rows)
        o_refs[i][...] = scratch[pl.ds(start, rows), :].astype(jnp.bfloat16)


def project(order, blocks, weights, base=None, tile=640):
    slots, pieces = len(blocks), len(weights)
    flat = [block for slot in blocks for block in slot]
    height, depth = flat[0].shape
    cols = weights[0][0].shape[1]
    rows = height // pieces
    chunks = [chunk for piece in weights for chunk in piece]
    based = base is not None
    a_specs = [pl.BlockSpec((rows, depth), lambda n, _, j=j: (j, 0)) for j in range(pieces)]
    w_specs = [pl.BlockSpec((chunk.shape[0], tile), lambda n, _: (0, n)) for chunk in chunks]
    whole = pl.BlockSpec((slots * rows, tile), lambda n, _: (0, n))
    part = pl.BlockSpec((rows, tile), lambda n, _: (0, n))
    if based:
        out_shape = [jax.ShapeDtypeStruct((rows, cols), jnp.bfloat16)] * slots
        scratch = [pltpu.VMEM((slots * rows, tile), jnp.float32)]
    else:
        out_shape = jax.ShapeDtypeStruct((slots * rows, cols), jnp.float32)
        scratch = []
    return pl.pallas_call(
        functools.partial(
            project_kernel,
            slots=[len(slot) for slot in blocks],
            chunks=[len(piece) for piece in weights],
            base=based,
        ),
        out_shape=out_shape,
        grid_spec=pltpu.PrefetchScalarGridSpec(
            num_scalar_prefetch=1,
            grid=(cols // tile,),
            in_specs=a_specs * len(flat) + w_specs + [whole] * based,
            out_specs=[part] * slots if based else whole,
            scratch_shapes=scratch,
        ),
        cost_estimate=pl.CostEstimate(
            flops=2 * slots * height * depth * cols,
            bytes_accessed=2 * pieces * depth * cols,
            transcendentals=0,
        ),
        name="project",
    )(
        order,
        *[block for block in flat for _ in range(pieces)],
        *chunks,
        *([base] if based else []),
    )


FIRST = [(0, 1), (1, 0), (2, 3), (3, 2)]
MIDDLE = [(1, 2), (2, 1)]
OUTWARD = [(1, 0), (2, 3)]


def xor(step, size=4):
    return [(i, i ^ step) for i in range(size)]


def after(value, *others):
    return lax.optimization_barrier((value,) + others)[0]


def pick(index, arrays):
    a, b, c, d = arrays
    return jnp.where(index < 2, jnp.where(index == 0, a, b), jnp.where(index == 2, c, d))


def four_planes(*args):
    return planes(*args)


def planes(queries, keys, values, positions, out_weight):
    tok = queries.shape[0]
    depth = out_weight.shape[0] // 2
    c = lax.axis_index("ctx")
    t = lax.axis_index("tp")
    g = lax.axis_index("groups")
    middle = (c == 1) | (c == 2)
    steps = jnp.arange(4, dtype=jnp.int32)

    kv = jnp.concatenate([keys, values], axis=1)
    kv_far, kv_two, kv_one = [lax.ppermute(kv, "ctx", xor(j)) for j in (3, 2, 1)]
    pos_of = [lax.dynamic_slice_in_dim(positions, (c ^ j) * tok, tok) for j in range(4)]
    pieces = attend(
        queries, [kv, kv_one, kv_two, kv_far], pos_of[0], jnp.concatenate(pos_of), t ^ steps
    )

    lead = depth * 3 // 5
    halves = [
        lax.dynamic_slice_in_dim(out_weight, g * depth, lead),
        lax.dynamic_slice_in_dim(out_weight, g * depth + lead, depth - lead),
    ]
    mine = [lax.ppermute(halves[i], "tp", xor(2)) for i in (0, 1)]
    beside = lax.ppermute(out_weight, "tp", xor(1))

    given = [lax.ppermute(pieces[j], "tp", xor(j)) for j in (1, 2, 3)]

    def line_gather(block):
        near = lax.ppermute(block, "ctx", FIRST)
        over = lax.ppermute(block, "ctx", MIDDLE)
        far = lax.ppermute(near, "ctx", MIDDLE)
        out_near = lax.ppermute(over, "ctx", OUTWARD)
        out_far = lax.ppermute(far, "ctx", OUTWARD)
        return [[block], [near], [over, out_near], [far, out_far]], (far, out_near)

    first_block = jnp.concatenate([pieces[0], given[0]], axis=0)
    same_chip, first_hop = line_gather(first_block)
    given[1:] = [
        jnp.where(g == 0, p, jnp.concatenate([p[:, depth:], p[:, :depth]], axis=1))
        for p in after(given[1:], first_block)
    ]
    second_block = jnp.concatenate(given[1:], axis=0)
    other_chip, second_hop = line_gather(second_block)

    mine = [after(mine[0], pieces[0]), after(mine[1], other_chip[1][0])]
    theirs = [lax.ppermute(mine[i], "groups", xor(1, 2)) for i in (0, 1)]
    across = mine + theirs
    across[:2] = after(across[:2], *first_hop)
    across[2] = after(across[2], *second_hop)

    step = t ^ steps ^ c
    slot = jnp.where(step < 2, step, jnp.where(middle, 5 - step, step))
    base = project(slot, same_chip, [[out_weight], [beside]])
    across[3] = after(across[3], base)
    beyond = [lax.ppermute(w, "tp", xor(1)) for w in across]
    results = project(slot, other_chip, [across, beyond], base)
    got = [
        lax.ppermute(
            results[j],
            ("ctx", "tp"),
            [(p * 4 + i, (i ^ j) * 4 + p) for p in range(4) for i in range(4)],
        )
        for j in range(4)
    ]
    return jnp.concatenate([pick(c ^ q, got) for q in range(4)], axis=0)


def any_mesh(queries, keys, values, positions, out_weight):
    tok = queries.shape[0]
    kv_heads = keys.shape[1] // HEAD_SIZE
    query_group = QUERY_HEADS // KEY_VALUE_HEADS
    scale = HEAD_SIZE ** (-0.5)
    ctx_index = lax.axis_index("ctx")
    query_pos = lax.dynamic_slice_in_dim(positions, ctx_index * tok, tok)
    query_four = queries.reshape(tok, kv_heads, query_group, HEAD_SIZE)

    def attend_block(carry, key_block, value_block, key_pos):
        top, total, accum = carry
        count = key_block.shape[0]
        key_three = key_block.reshape(count, kv_heads, HEAD_SIZE)
        value_three = value_block.reshape(count, kv_heads, HEAD_SIZE)
        scores = (
            jnp.einsum("tgjd,kgd->gjtk", query_four, key_three, preferred_element_type=jnp.float32)
            * scale
        )
        keep = key_pos[None, :] <= query_pos[:, None]
        scores = jnp.where(keep, scores, -1e30)
        new_top = jnp.maximum(top, jnp.max(scores, axis=-1))
        factor = jnp.exp(top - new_top)
        expo = jnp.where(keep, jnp.exp(scores - new_top[..., None]), 0.0)
        total = total * factor + jnp.sum(expo, axis=-1)
        weights = expo.astype(jnp.bfloat16)
        accum = accum * factor[..., None] + jnp.einsum(
            "gjtk,kgd->gjtd", weights, value_three, preferred_element_type=jnp.float32
        )
        return (new_top, total, accum)

    start_top = jnp.full((kv_heads, query_group, tok), -1e30, jnp.float32)
    start_total = jnp.zeros((kv_heads, query_group, tok), jnp.float32)
    start_accum = jnp.zeros((kv_heads, query_group, tok, HEAD_SIZE), jnp.float32)
    key_piece = lax.all_gather(keys, "ctx", axis=0, tiled=True)
    value_piece = lax.all_gather(values, "ctx", axis=0, tiled=True)
    rows = key_piece.shape[0]
    width = math.gcd(rows, 512)

    def step(index, state):
        offset = index * width
        key_block = lax.dynamic_slice_in_dim(key_piece, offset, width, 0)
        value_block = lax.dynamic_slice_in_dim(value_piece, offset, width, 0)
        key_pos = lax.dynamic_slice_in_dim(positions, offset, width, 0)
        return attend_block(state, key_block, value_block, key_pos)

    _, total, accum = lax.fori_loop(0, rows // width, step, (start_top, start_total, start_accum))
    attended = (
        (accum / total[..., None])
        .transpose(2, 0, 1, 3)
        .reshape(tok, kv_heads * query_group * HEAD_SIZE)
        .astype(jnp.bfloat16)
    )
    partial_value = jnp.dot(
        attended,
        lax.all_gather(out_weight, "ctx", axis=1, tiled=True),
        preferred_element_type=jnp.float32,
    )
    return lax.psum_scatter(
        partial_value.astype(jnp.bfloat16), "tp", scatter_dimension=1, tiled=True
    )


def solution(mesh):
    square = mesh.shape["ctx"] == 4 and mesh.shape["tp"] == 4
    return jax.shard_map(
        four_planes if square else any_mesh,
        mesh=mesh,
        in_specs=(
            P(("groups", "ctx"), "tp"),
            P(("groups", "ctx"), "tp"),
            P(("groups", "ctx"), "tp"),
            P("groups"),
            P("tp", "ctx"),
        ),
        out_specs=P(("groups", "ctx"), "tp"),
        check_vma=False,
    )
```
